32 devices in a mesh: gx: 4 (over z), gy: 2 (over y), gz: 4 (over x, core).
Axes of the slice: x: 2, y: 2, z: 4, core: 2. Of those that a mesh axis runs over, the one named last changes fastest.
Arguments:
- nodal_warmth_degrees: float32 [3, 3, 3, 16, 8, 512], P(None, None, None, 'gx', 'gy', 'gz'), may hold values from -6 to 6
- thermal_transfer_coefficient: float32 [16, 8, 512], P('gx', 'gy', 'gz'), may hold values from 0.1 to 2
- taken_beam_fraction: float32 [16, 8, 512], P('gx', 'gy', 'gz'), may hold values from 0.3 to 3
- laid_tiers: int32 [4, 2, 4], P('gx', 'gy', 'gz'), may hold values from 64 to 128
- holding_brick_column: int32 [4, 2, 4, 2048, 1], P('gx', 'gy', 'gz'), may hold values from 0 to 3; in each aligned block of 2048 rows (0 to 2047, 2048 to 4095, ..., all dimensions but the last counted through in order) at most 1024 rows name the same one
- piece_onto_solid_brick: int32 [4, 2, 4, 2048], P('gx', 'gy', 'gz'), may hold values from 0 to 255, as said below
- deformation_change: float32 [6, 8, 8192], P(None, None, ('gx', 'gy', 'gz')), may hold values from -0.06 to 0.06
- earlier_tension_state: float32 [6, 8, 8192], P(None, None, ('gx', 'gy', 'gz')), may hold values from -3 to 3
- plastic_onset_threshold: float32 [8192], P(('gx', 'gy', 'gz')), may hold values from 0.5 to 2
Outputs:
- temperature_new: float32 [3, 3, 3, 16, 8, 512], P(None, None, None, 'gx', 'gy', 'gz')
- stress_new: float32 [6, 8, 8192], P(None, None, ('gx', 'gy', 'gz'))
- forces: float32 [3, 8, 8192], P(None, None, ('gx', 'gy', 'gz'))
The draws below stay inside these ranges and needn't reach their ends.
Inputs may be any that keep to these rules, and one draw needn't show every extreme that they name: `holding_brick_column`: the elements of one device hand at most 1024 elements to one owner; in every draw some device hands exactly 1024 to some owner. `piece_onto_solid_brick`: some mechanical cells may receive no element.
All inputs are finite; a program needn't handle non-finite values.
Results may differ from the reference program's by a relative error of at most 0.00022.
Values sent between devices are 32-bit elements; how exact they have to be, the bound alone decides.
A program may use at most 64 MiB of HBM per device.

```python
import math
import jax
import jax.numpy as jnp
import numpy as np
from jax import lax

PART_PIECES_LONG = 4
PART_PIECES_WIDE = 4
PART_PIECES_TALL = 128
STEPS = 4
PLATE_PIECES_LONG = 16
PLATE_PIECES_WIDE = 8
PLATE_PIECES_TALL = 512
ELEM_DEV = 2048
CAP = 1024
MC_DEV = 256
MC_TOTAL = 8192
N_GX = 4
N_GY = 2
N_GZ = 4


def draw_piece_onto_solid_brick(key, part):
    empty_cell = jax.random.randint(jax.random.fold_in(key, 11), (1, N_GY, N_GZ, 1), 0, MC_DEV)
    drawn = jax.random.randint(jax.random.fold_in(key, 12), (N_GX, N_GY, N_GZ, ELEM_DEV), 0, MC_DEV - 1)
    return (drawn + (drawn >= empty_cell).astype(jnp.int32)).astype(jnp.int32)


def plant(result, stream_key, smallest, top_value):
    spot = [jax.random.randint(jax.random.fold_in(stream_key, axis), (), 0, length) for axis, length in enumerate(result.shape)]
    longest = result.shape.index(max(result.shape))
    neighbour = spot[:longest] + [(spot[longest] + 1) % result.shape[longest]] + spot[longest + 1:]
    return result.at[tuple(spot)].set(smallest).at[tuple(neighbour)].set(top_value)


def levels(own_key, shape, shards, least, high):
    level = 1.0
    for position, blocks in shards:
        draws = jax.random.uniform(jax.random.fold_in(jax.random.fold_in(own_key, 6), position), (blocks,), jnp.float32, least / len(shards), high / len(shards))
        level = level * jnp.repeat(jnp.exp(draws), shape[position] // blocks).reshape((-1,) + (1,) * (len(shape) - 1 - position))
    return level


def deal_out(stream_key, own, number, rows, number_of, top, most, lean):
    order = jax.random.permutation(stream_key, number_of)
    packed, ordinary = load_shares(number_of, rows * top, most, lean, True), load_shares(number_of, rows * top, most, lean, False)
    places = jnp.arange(number_of)

    def named(lengths, rotation):
        used = int((lengths > 0).sum())
        fixed = max(1, used // 4)
        shifted = fixed + (places - fixed + rotation * (used - fixed)) % max(1, number_of - fixed)
        return jnp.zeros((number_of,), jnp.int32).at[order[jnp.where(places < fixed, places, shifted)]].set(jnp.asarray(lengths, jnp.int32))

    lengths = jnp.where(number % 4 == 0, named(packed, number // 4), named(ordinary, number - number // 4 - 1))
    mixed = jax.random.permutation(jax.random.fold_in(own, 3), number_of)
    donor, sink = mixed[0:number_of // 2 * 2:2], mixed[1:number_of // 2 * 2:2]
    margin = jnp.minimum(lengths[donor] - 1, most - lengths[sink]) // 2
    margin = jnp.where((donor == order[0]) | (sink == order[0]) | (lengths[sink] == 0), 0, jnp.maximum(margin, 0))
    shifted = jax.random.randint(jax.random.fold_in(own, 4), (number_of // 2,), 0, 1 << 20) % (margin + 1)
    lengths = lengths.at[donor].add(-shifted).at[sink].add(shifted)
    items = jnp.searchsorted(jnp.cumsum(lengths), jnp.arange(rows * top), side="right").astype(jnp.int32)
    table = items.reshape(top, rows).T
    table = table[jax.random.permutation(jax.random.fold_in(own, 1), rows)]
    rotation = jax.random.randint(jax.random.fold_in(own, 2), (rows, 1), 0, top)
    return jnp.take_along_axis(table, (jnp.arange(top)[None, :] + rotation) % top, axis=1)


def load_shares(number_of, total, bound, skew, full):
    loads = [(1 << 20) // math.isqrt(grade ** skew) + 1 for grade in range(1, number_of + 1)]
    largest = bound if full else min(bound, max(-(-total // number_of), total * loads[0] // sum(loads)))
    least = 1 if total - largest >= number_of - 1 else 0
    given, spare = [largest] + [least] * (number_of - 1), total - largest - least * (number_of - 1)
    while spare > 0:
        movable = [i for i in range(1, number_of) if given[i] < largest] or [i for i in range(1, number_of) if given[i] < bound]
        pool, remaining = sum([loads[i] for i in movable]), spare
        for i in movable:
            more = min(bound - given[i], max(1, remaining * loads[i] // pool), spare)
            given[i] = given[i] + more
            spare = spare - more
    return np.array(given)


def normal_values(rng, dims, scale, bound, split=(), held_as=jnp.bfloat16):
    entries = jax.random.normal(rng, dims, jnp.float32) * scale
    if len(split) > 0:
        entries = levels(rng, dims, split, -0.22, 0.18) * entries
    return jnp.clip(entries, min=-bound, max=bound).astype(held_as)


def setup_inputs(seed: int = 0) -> dict:
    key_of = jax.random.split(jax.random.key(seed), 10)
    nodal_warmth_degrees = normal_values(key_of[0], (3, 3, 3, PLATE_PIECES_LONG, PLATE_PIECES_WIDE, PLATE_PIECES_TALL), 1.0, 6.0, ((3, 4), (4, 2), (5, 4)), jnp.float32)
    thermal_transfer_coefficient = jnp.clip(jnp.exp(math.log(2.0) - 2.9957323 * jax.random.uniform(key_of[1], (PLATE_PIECES_LONG, PLATE_PIECES_WIDE, PLATE_PIECES_TALL), jnp.float32) ** levels(key_of[1], (PLATE_PIECES_LONG, PLATE_PIECES_WIDE, PLATE_PIECES_TALL), ((0, 4), (1, 2), (2, 4)), -0.2, 0.2)), 0.1, 2.0)
    taken_beam_fraction = jnp.clip(jnp.exp(math.log(3.0) - 2.3025851 * jax.random.uniform(key_of[2], (PLATE_PIECES_LONG, PLATE_PIECES_WIDE, PLATE_PIECES_TALL), jnp.float32) ** levels(key_of[2], (PLATE_PIECES_LONG, PLATE_PIECES_WIDE, PLATE_PIECES_TALL), ((0, 4), (1, 2), (2, 4)), -0.2, 0.2)), 0.3, 3.0)
    laid_tiers = plant(jax.random.randint(key_of[3], (N_GX, N_GY, N_GZ), PART_PIECES_TALL // 2, PART_PIECES_TALL + 1), jax.random.fold_in(key_of[3], 1), PART_PIECES_TALL // 2, PART_PIECES_TALL).astype(jnp.int32)
    holding_brick_column_keys = jax.random.split(jax.random.fold_in(key_of[4], 1), N_GX * N_GY * N_GZ * ELEM_DEV // ELEM_DEV)
    holding_brick_column_turns = jax.random.permutation(jax.random.fold_in(key_of[4], 3), N_GX * N_GY * N_GZ * ELEM_DEV // ELEM_DEV)
    holding_brick_column = jax.vmap(lambda own, number: deal_out(jax.random.fold_in(key_of[4], 2), own, number, ELEM_DEV, N_GX, 1, CAP, 2))(holding_brick_column_keys, holding_brick_column_turns).reshape((N_GX, N_GY, N_GZ, ELEM_DEV, 1))
    piece_onto_solid_brick = draw_piece_onto_solid_brick(jax.random.fold_in(key_of[9], 71), 0)
    deformation_change = normal_values(key_of[6], (6, 8, MC_TOTAL), 0.01, 0.06, ((2, 32),), jnp.float32)
    earlier_tension_state = normal_values(key_of[7], (6, 8, MC_TOTAL), 0.5, 3.0, ((2, 32),), jnp.float32)
    plastic_onset_threshold = jnp.clip(jnp.exp(math.log(2.0) - 1.3862944 * jax.random.uniform(key_of[8], (MC_TOTAL,), jnp.float32) ** levels(key_of[8], (MC_TOTAL,), ((0, 32),), -0.2, 0.2)), 0.5, 2.0)
    return dict(nodal_warmth_degrees=nodal_warmth_degrees, thermal_transfer_coefficient=thermal_transfer_coefficient, taken_beam_fraction=taken_beam_fraction, laid_tiers=laid_tiers, holding_brick_column=holding_brick_column, piece_onto_solid_brick=piece_onto_solid_brick, deformation_change=deformation_change, earlier_tension_state=earlier_tension_state, plastic_onset_threshold=plastic_onset_threshold)


time_step = 0.003
penalty = 3.0
heat_power = 100.0
expansion = 0.02
shear_modulus = 100.0 / 2.6
lame_first = 30.0 / 0.52
hardening = 10.0
highest = lax.Precision.HIGHEST
nodal_weights = np.array([1.0 / 6.0, 2.0 / 3.0, 1.0 / 6.0], np.float32)

def lumped_line():
    stiff = np.array([[7.0, -8.0, 1.0], [-8.0, 16.0, -8.0], [1.0, -8.0, 7.0]], np.float32) / 3.0
    return stiff / nodal_weights[:, None]

def gauss_spots():
    half = 0.5 / math.sqrt(3.0)
    return [0.5 - half, 0.5 + half]

def gauss_values():
    rows = []
    for point in gauss_spots():
        rows.append([2.0 * (point - 0.5) * (point - 1.0), -4.0 * point * (point - 1.0), 2.0 * point * (point - 0.5)])
    return np.array(rows, np.float32)

def gradient_table():
    spots = gauss_spots()
    table = np.zeros((3, 8, 8), np.float32)
    for node in range(8):
        corner = [node // 4, node // 2 % 2, node % 2]
        for point in range(8):
            place = [spots[point // 4], spots[point // 2 % 2], spots[point % 2]]
            values = [place[k] if corner[k] else 1.0 - place[k] for k in range(3)]
            slopes = [1.0 if corner[k] else -1.0 for k in range(3)]
            table[0, node, point] = slopes[0] * values[1] * values[2] / 8.0
            table[1, node, point] = values[0] * slopes[1] * values[2] / 8.0
            table[2, node, point] = values[0] * values[1] * slopes[2] / 8.0
    return table

def window(array, lead, axis, offset):
    index = [slice(None)] * lead
    for k in range(3):
        move = offset if k == axis else 0
        index.append(slice(1 + move, array.shape[lead + k] - 1 + move))
    return array[tuple(index)]

def node_terms(anchor, count, centre, near, far):
    places = (jnp.arange(count) + anchor).astype(jnp.float32)[None, :] + 0.5 * jnp.arange(3).astype(jnp.float32)[:, None]
    offset = places - centre
    radius = jnp.where(offset >= 0.0, near, far)
    return -3.0 * (offset / radius) ** 2

def advance_solution(nodal_quantity_entries, diffusivity, mask, absorb_heat, anchor, step_forward, extent):
    core = window(nodal_quantity_entries, 3, 0, 0)
    kcore = window(diffusivity, 0, 0, 0)
    mcore = window(mask, 0, 0, 0)
    acore = window(absorb_heat, 0, 0, 0)
    line = jnp.asarray(lumped_line())
    rate = jnp.einsum('ai,ibcxyz->abcxyz', line, core, precision=highest)
    rate = rate + jnp.einsum('bi,aicxyz->abcxyz', line, core, precision=highest)
    rate = rate + jnp.einsum('ci,abixyz->abcxyz', line, core, precision=highest)
    rate = -kcore * rate
    for axis in range(3):
        for offset, own, other in ((1, 2, 0), (-1, 0, 2)):
            beside = window(nodal_quantity_entries, 3, axis, offset)
            kbeside = window(diffusivity, 0, axis, offset)
            mbeside = window(mask, 0, axis, offset)
            couple = penalty * 2.0 * kcore * kbeside / jnp.maximum(kcore + kbeside, 1.0) * mcore * mbeside
            jump = jnp.take(core, own, axis=axis) - jnp.take(beside, other, axis=axis)
            flux = couple * jump / float(nodal_weights[own])
            rate = rate.at[(slice(None),) * axis + (own,)].add(-flux)
    length, width, height = extent
    shape = core.shape
    xterm = node_terms(anchor[0], shape[3], length * 0.5 + step_forward * length / 16.0, length / 8.0, length / 4.0)
    yterm = node_terms(anchor[1], shape[4], width * 0.5, width / 4.0, width / 4.0)
    zterm = node_terms(anchor[2], shape[5], height * 0.75, height / 8.0, height / 8.0)
    total = xterm[:, None, None, :, None, None] + yterm[None, :, None, None, :, None] + zterm[None, None, :, None, None, :]
    source = heat_power * (2.0 / 3.0) * jnp.exp(total) * acore
    return core + time_step * mcore * (rate + source)

def gauss_point_change(change):
    table = jnp.asarray(gauss_values())
    value = jnp.einsum('pa,abcxyz->pbcxyz', table, change, precision=highest)
    value = jnp.einsum('qb,pbcxyz->pqcxyz', table, value, precision=highest)
    value = jnp.einsum('rc,pqcxyz->pqrxyz', table, value, precision=highest)
    return value

def mechanics(deformation_change, earlier_tension_state, plastic_onset_threshold, thermal):
    normal_component = deformation_change[0:3] - expansion * thermal[None]
    volume = normal_component[0] + normal_component[1] + normal_component[2]
    trial_normal = earlier_tension_state[0:3] + lame_first * volume[None] + 2.0 * shear_modulus * normal_component
    trial_shear = earlier_tension_state[3:6] + 2.0 * shear_modulus * deformation_change[3:6]
    pressure = (trial_normal[0] + trial_normal[1] + trial_normal[2]) / 3.0
    dev_normal = trial_normal - pressure[None]
    squares = lax.optimization_barrier(jnp.sum(dev_normal * dev_normal, axis=0)) + 2.0 * lax.optimization_barrier(jnp.sum(trial_shear * trial_shear, axis=0))
    equivalent = jnp.sqrt(1.5 * squares)
    limit = plastic_onset_threshold[None, :]
    plastic = jnp.maximum(equivalent - limit, 0.0) / (3.0 * shear_modulus + hardening)
    factor = 1.0 - 3.0 * shear_modulus * plastic / jnp.maximum(equivalent, limit)
    new_normal = pressure[None] + factor[None] * dev_normal
    new_shear = factor[None] * trial_shear
    stress_new = jnp.concatenate([new_normal, new_shear], axis=0)
    rows = [[0, 5, 4], [5, 1, 3], [4, 3, 2]]
    tensor = jnp.stack([jnp.stack([stress_new[k] for k in row], axis=0) for row in rows], axis=0)
    forces = jnp.einsum('dig,cdgm->cim', jnp.asarray(gradient_table()), tensor, precision=highest)
    return (stress_new, forces)

def reference(nodal_warmth_degrees, thermal_transfer_coefficient, taken_beam_fraction, laid_tiers, holding_brick_column, piece_onto_solid_brick, deformation_change, earlier_tension_state, plastic_onset_threshold):
    full_layers = jnp.repeat(jnp.repeat(jnp.repeat(laid_tiers, PART_PIECES_LONG, axis=0), PART_PIECES_WIDE, axis=1), PART_PIECES_TALL, axis=2)
    device_height = jnp.arange(PLATE_PIECES_TALL) % PART_PIECES_TALL
    mask = (device_height[None, None, :] < full_layers).astype(jnp.float32)

    def cycle_index(array, lead):
        return jnp.pad(array, [(0, 0)] * lead + [(1, 1)] * 3)
    diffusivity = cycle_index(thermal_transfer_coefficient, 0)
    masked_values = cycle_index(mask, 0)
    absorb_heat = cycle_index(taken_beam_fraction, 0)
    nodal_quantity_entries = nodal_warmth_degrees
    for step_forward in range(STEPS):
        nodal_quantity_entries = advance_solution(cycle_index(nodal_quantity_entries, 3), diffusivity, masked_values, absorb_heat, (0, 0, 0), step_forward, (PLATE_PIECES_LONG, PLATE_PIECES_WIDE, PLATE_PIECES_TALL))
    change_amount_entry = gauss_point_change(nodal_quantity_entries - nodal_warmth_degrees).reshape(8, N_GX, PART_PIECES_LONG, N_GY, PART_PIECES_WIDE, N_GZ, PART_PIECES_TALL)
    change_amount_entry = jnp.transpose(change_amount_entry, (0, 1, 3, 5, 2, 4, 6)).reshape(8, -1)
    weights = jnp.transpose(mask.reshape(N_GX, PART_PIECES_LONG, N_GY, PART_PIECES_WIDE, N_GZ, PART_PIECES_TALL), (0, 2, 4, 1, 3, 5)).reshape(-1)
    row_y = jnp.arange(N_GY).astype(jnp.int32)[None, :, None, None]
    row_z = jnp.arange(N_GZ).astype(jnp.int32)[None, None, :, None]
    target = ((holding_brick_column[..., 0] * N_GY + row_y) * N_GZ + row_z) * MC_DEV + piece_onto_solid_brick
    target = target.reshape(-1).astype(jnp.int32)
    sums = jnp.zeros((8, MC_TOTAL), jnp.float32).at[:, target].add(change_amount_entry * weights[None, :])
    counts = jnp.zeros((MC_TOTAL,), jnp.float32).at[target].add(weights)
    thermal = sums / jnp.maximum(counts, 1.0)[None, :]
    stress_new, forces = mechanics(deformation_change, earlier_tension_state, plastic_onset_threshold, thermal)
    return (nodal_quantity_entries, stress_new, forces)
```

```python
import functools
import math

import jax
import jax.numpy as jnp
from jax import lax
from jax.experimental import pallas as pl
from jax.experimental.pallas import tpu as pltpu
from jax.sharding import PartitionSpec as P

STEPS = 4

time_step = 0.003
penalty = 3.0
heat_power = 100.0
expansion = 0.02
shear_modulus = 100.0 / 2.6
lame_first = 30.0 / 0.52
hardening = 10.0
LANES = 128
GROUP = 8
MESH = pl.DeviceIdType.MESH


def face_planes(axis, side):
    planes = []
    for first in range(3):
        for second in range(3):
            index = [first, second]
            index.insert(axis, side)
            planes.append(9 * index[0] + 3 * index[1] + index[2])
    return planes


def gauss_rows():
    half = 0.5 / math.sqrt(3.0)
    return [
        [2.0 * (g - 0.5) * (g - 1.0), -4.0 * g * (g - 1.0), 2.0 * g * (g - 0.5)]
        for g in (0.5 - half, 0.5 + half)
    ]


def pair_coefficient(own, beside):
    scale = time_step * penalty * 2.0 * 6.0
    return scale * own * beside / jnp.maximum(own + beside, 1.0)


def kernel(
    block,
    counts_of,
    cells,
    tiers,
    warm_hbm,
    cond_hbm,
    beam_hbm,
    owner_hbm,
    piece_hbm,
    strain_hbm,
    stress_hbm,
    limit_hbm,
    temp_out,
    stress_out,
    forces_out,
    warm,
    cond,
    beam,
    owner,
    piece,
    strain,
    stress,
    limit,
    ping,
    pong,
    send_x,
    send_y,
    send_z,
    got_x,
    got_y,
    got_z,
    points,
    spread,
    hot,
    outbox,
    inbox,
    new_stress,
    new_forces,
    in_sems,
    out_sems,
    halo_send,
    halo_recv,
    trade_send,
    trade_recv,
):
    size_x, size_y, size_z = block
    rows = size_x * size_y
    names = ("gx", "gy", "gz")
    places = tuple(lax.axis_index(name) for name in names)
    has_lower = tuple(place > 0 for place in places)
    has_upper = tuple(place < count - 1 for place, count in zip(places, counts_of))
    peers = counts_of[0]
    chunks = cells // LANES
    slots = peers * chunks

    loads = [
        pltpu.make_async_copy(source, target, in_sems.at[index])
        for index, (source, target) in enumerate(
            (
                (warm_hbm, warm),
                (cond_hbm, cond),
                (beam_hbm, beam),
                (owner_hbm, owner),
                (piece_hbm, piece),
                (strain_hbm, strain),
                (stress_hbm, stress),
                (limit_hbm, limit),
            )
        )
    ]
    for load in loads:
        load.start()

    barrier = pltpu.get_barrier_semaphore()
    for shift in range(1, peers):
        pl.semaphore_signal(
            barrier, inc=1, device_id={"gx": lax.rem(places[0] + shift, peers)}, device_id_type=MESH
        )
    for axis in (1, 2):
        for exists, move in ((has_lower[axis], -1), (has_upper[axis], 1)):

            @pl.when(exists)
            def _(axis=axis, move=move):
                pl.semaphore_signal(
                    barrier, inc=1, device_id={names[axis]: places[axis] + move}, device_id_type=MESH
                )

    sends = (send_x, send_y, send_z)
    gots = (got_x, got_y, got_z)

    for axis in range(3):
        for exists, side in ((has_lower[axis], 0), (has_upper[axis], 1)):

            @pl.when(jnp.logical_not(exists))
            def _(axis=axis, side=side):
                gots[axis][:, side] = jnp.zeros(gots[axis].shape[:1] + gots[axis].shape[2:], jnp.float32)

    def halo(step, axis, up):
        index = (step * 3 + axis) * 2
        target = places[axis] + (1 if up else -1)
        return pltpu.make_async_remote_copy(
            src_ref=sends[axis].at[step, 1 if up else 0],
            dst_ref=gots[axis].at[step, 0 if up else 1],
            send_sem=halo_send.at[index + (1 if up else 0)],
            recv_sem=halo_recv.at[index + (0 if up else 1)],
            device_id={names[axis]: target},
            device_id_type=MESH,
        )

    lane = lax.broadcasted_iota(jnp.int32, (rows, LANES), 1)
    row = lax.broadcasted_iota(jnp.int32, (rows, LANES), 0)
    row_x = row // size_y
    row_y = row - row_x * size_y

    for load in loads[:3]:
        load.wait()
    mask = (lane < tiers[0, 0]).astype(jnp.float32)
    flow = cond[...] * mask

    send_x[0, 0, 9 * size_y : 10 * size_y] = flow[:size_y]
    send_x[0, 1, 9 * size_y : 10 * size_y] = flow[rows - size_y :]
    hold = pong
    hold[0:rows] = flow
    send_y[0, 0, 9 * size_x : 10 * size_x] = hold[pl.ds(0, size_x, stride=size_y)]
    send_y[0, 1, 9 * size_x : 10 * size_x] = hold[pl.ds(size_y - 1, size_x, stride=size_y)]

    neighbours = peers - 1
    for axis in (1, 2):
        neighbours = neighbours + has_lower[axis].astype(jnp.int32) + has_upper[axis].astype(jnp.int32)

    def pack(current, step):
        for side, face in ((0, 0), (1, 2)):
            first = 0 if side == 0 else rows - size_y
            for v, plane in enumerate(face_planes(0, face)):
                send_x[step, side, v * size_y : (v + 1) * size_y] = current[
                    plane * rows + first : plane * rows + first + size_y
                ]
            first = 0 if side == 0 else size_y - 1
            for v, plane in enumerate(face_planes(1, face)):
                send_y[step, side, v * size_x : (v + 1) * size_x] = current[
                    pl.ds(plane * rows + first, size_x, stride=size_y)
                ]
            first = 0 if side == 0 else LANES - 1
            packed = None
            for v, plane in enumerate(face_planes(2, face)):
                value = current[plane * rows : (plane + 1) * rows]
                shift = (v - first) % LANES
                value = pltpu.roll(value, shift, 1) if shift else value
                packed = value if packed is None else jnp.where(lane == v, value, packed)
            if step == 0:
                shift = (9 - first) % LANES
                packed = jnp.where(lane == 9, pltpu.roll(flow, shift, 1), packed)
            send_z[step, side] = packed

    def start(step):
        for axis in range(3):
            for up, exists in ((False, has_lower[axis]), (True, has_upper[axis])):

                @pl.when(exists)
                def _(axis=axis, up=up):
                    halo(step, axis, up).start()

    def arrive(step):
        for axis in range(3):
            for up, exists in ((False, has_upper[axis]), (True, has_lower[axis])):

                @pl.when(exists)
                def _(axis=axis, up=up):
                    halo(step, axis, up).wait_recv()

    pack(warm, 0)
    pl.semaphore_wait(barrier, neighbours)
    start(0)

    def inner(value, axis):
        if axis == 0:
            down, up = pltpu.roll(value, size_y, 0), pltpu.roll(value, rows - size_y, 0)
            low, high = row_x == 0, row_x == size_x - 1
        elif axis == 1:
            down, up = pltpu.roll(value, 1, 0), pltpu.roll(value, rows - 1, 0)
            low, high = row_y == 0, row_y == size_y - 1
        else:
            down, up = pltpu.roll(value, 1, 1), pltpu.roll(value, LANES - 1, 1)
            low, high = lane == 0, lane == LANES - 1
        return (
            jnp.where(low, 0.0, pair_coefficient(value, down)),
            jnp.where(high, 0.0, pair_coefficient(value, up)),
        )

    couples = [inner(flow, axis) for axis in range(3)]
    through = time_step * flow
    extent = [size * count for size, count in zip(block, counts_of)]
    begin = [(place * size) for place, size in zip(places, block)]

    def bell(where, node, centre, near, far):
        offset = where + 0.5 * node - centre
        ratio = offset / jnp.where(offset >= 0.0, near, far)
        return jnp.exp(-3.0 * ratio * ratio)

    where_x = (row_x + begin[0]).astype(jnp.float32)
    where_y = (row_y + begin[1]).astype(jnp.float32)
    where_z = (lane + begin[2]).astype(jnp.float32)
    length, width, height = extent
    heat = (time_step * heat_power * (2.0 / 3.0)) * mask * beam[...]
    bell_y = [bell(where_y, node, width * 0.5, width / 4.0, width / 4.0) for node in range(3)]
    bell_z = [
        heat * bell(where_z, node, height * 0.75, height / 8.0, height / 8.0) for node in range(3)
    ]

    def advance(current, following, step):
        bell_x = [
            bell(
                where_x,
                node,
                length * 0.5 + step * length / 16.0,
                length / 8.0,
                length / 4.0,
            )
            for node in range(3)
        ]
        for part in range(rows // GROUP):
            cut = slice(part * GROUP, (part + 1) * GROUP)
            t = [
                current[plane * rows + part * GROUP : plane * rows + (part + 1) * GROUP]
                for plane in range(27)
            ]
            rate = [None] * 27
            for axis in range(3):
                for v in range(9):
                    p0, p1, p2 = (face_planes(axis, k)[v] for k in range(3))
                    d0, d2 = t[p0] - t[p1], t[p2] - t[p1]
                    both = 2.0 * (d0 + d2)
                    for plane, term in (
                        (p0, both + 12.0 * d0),
                        (p1, -2.0 * both),
                        (p2, both + 12.0 * d2),
                    ):
                        rate[plane] = term if rate[plane] is None else rate[plane] + term
            for a in range(3):
                for b in range(3):
                    beam_ab = bell_x[a][cut] * bell_y[b][cut]
                    for c in range(3):
                        plane = 9 * a + 3 * b + c
                        value = t[plane] - through[cut] * rate[plane] + beam_ab * bell_z[c][cut]
                        following[plane * rows + part * GROUP : plane * rows + (part + 1) * GROUP] = value
        for axis in range(3):
            along = 1 if axis == 2 else 0
            span = LANES if axis == 2 else rows
            shift = (size_y, 1, 1)[axis]
            for p0, p2 in zip(face_planes(axis, 0), face_planes(axis, 2)):
                s0 = slice(p0 * rows, (p0 + 1) * rows)
                s2 = slice(p2 * rows, (p2 + 1) * rows)
                bottom, top = current[s0], current[s2]
                following[s0] += couples[axis][0] * (pltpu.roll(top, shift, along) - bottom)
                following[s2] += couples[axis][1] * (pltpu.roll(bottom, span - shift, along) - top)

    def fix(current, following, step, edges):
        for side, face in ((0, 0), (1, 2)):
            first = 0 if side == 0 else rows - size_y
            for v, plane in enumerate(face_planes(0, face)):
                at = slice(plane * rows + first, plane * rows + first + size_y)
                beside = got_x[step, side, v * size_y : (v + 1) * size_y]
                following[at] += edges[0][side] * (beside - current[at])
            first = 0 if side == 0 else size_y - 1
            for v, plane in enumerate(face_planes(1, face)):
                at = pl.ds(plane * rows + first, size_x, stride=size_y)
                beside = got_y[step, side, v * size_x : (v + 1) * size_x]
                following[at] = following[at] + edges[1][side] * (beside - current[at])
            first = 0 if side == 0 else LANES - 1
            packed = got_z[step, side]
            for v, plane in enumerate(face_planes(2, face)):
                at = slice(plane * rows, (plane + 1) * rows)
                shift = (first - v) % LANES
                beside = pltpu.roll(packed, shift, 1) if shift else packed
                following[at] += edges[2][side] * (beside - current[at])

    def outer_couples():
        points[0:rows] = flow
        edges = []
        edges.append(
            [
                pair_coefficient(
                    flow[first : first + size_y], got_x[0, side, 9 * size_y : 10 * size_y]
                )
                for side, first in ((0, 0), (1, rows - size_y))
            ]
        )
        edges.append(
            [
                pair_coefficient(
                    points[pl.ds(first, size_x, stride=size_y)],
                    got_y[0, side, 9 * size_x : 10 * size_x],
                )
                for side, first in ((0, 0), (1, size_y - 1))
            ]
        )
        edges.append(
            [
                jnp.where(
                    lane == first,
                    pair_coefficient(flow, pltpu.roll(got_z[0, side], (first - 9) % LANES, 1)),
                    0.0,
                )
                for side, first in ((0, 0), (1, LANES - 1))
            ]
        )
        return edges

    def label_rows():
        for load in loads[3:5]:
            load.wait()
        low_iota = lax.broadcasted_iota(jnp.int32, (LANES, LANES), 0)
        slot_iota = lax.broadcasted_iota(jnp.int32, (slots, LANES), 0)
        cell = piece[...]
        chunk = cell // LANES
        low = cell - chunk * LANES
        slot = jnp.where(lane < tiers[0, 0], owner[...] * chunks + chunk, -1)
        for r in range(rows):
            at = slice(r * LANES, (r + 1) * LANES)
            hot[:, at] = (low_iota == low[r : r + 1]).astype(jnp.float32).astype(jnp.bfloat16)
            spread[slots * 2 * GROUP :, at] = (
                (slot_iota == slot[r : r + 1]).astype(jnp.float32).astype(jnp.bfloat16)
            )
        return slot

    slot = None
    edges = None
    current = warm
    for step in range(STEPS):
        following = ping if step % 2 == 0 else pong
        if step > 0:
            pack(current, step)
            start(step)
        advance(current, following, step)
        if step == 0:
            slot = label_rows()
        arrive(step)
        if step == 0:
            edges = outer_couples()
        fix(current, following, step, edges)
        current = following

    write_temp = pltpu.make_async_copy(current, temp_out, out_sems.at[0])
    write_temp.start()

    table = gauss_rows()
    for part in range(rows // GROUP):
        change = [
            current[p * rows + part * GROUP : p * rows + (part + 1) * GROUP]
            - warm[p * rows + part * GROUP : p * rows + (part + 1) * GROUP]
            for p in range(27)
        ]
        stage = [
            [sum(table[p][a] * change[9 * a + v] for a in range(3)) for v in range(9)] for p in range(2)
        ]
        stage = [
            [
                [sum(table[q][b] * stage[p][3 * b + c] for b in range(3)) for c in range(3)]
                for q in range(2)
            ]
            for p in range(2)
        ]
        for p in range(2):
            for q in range(2):
                for r in range(2):
                    g = 4 * p + 2 * q + r
                    points[g * rows + part * GROUP : g * rows + (part + 1) * GROUP] = sum(
                        table[r][c] * stage[p][q][c] for c in range(3)
                    )

    for r in range(rows):
        at = slice(r * LANES, (r + 1) * LANES)
        value = points[pl.ds(r, GROUP, stride=rows)]
        coarse = value.astype(jnp.bfloat16).astype(jnp.float32)
        both = jnp.concatenate([coarse, value - coarse], axis=0)
        mine = jnp.broadcast_to(slot[r : r + 1], (2 * GROUP, LANES))
        for s in range(slots):
            spread[s * 2 * GROUP : (s + 1) * 2 * GROUP, at] = jnp.where(mine == s, both, 0.0).astype(
                jnp.bfloat16
            )
    total = lax.dot_general(
        spread[...], hot[...], (((1,), (1,)), ((), ())), preferred_element_type=jnp.float32
    )
    for o in range(peers):
        for k in range(chunks):
            s = o * chunks + k
            outbox[o, k * GROUP : (k + 1) * GROUP] = (
                total[s * 2 * GROUP : s * 2 * GROUP + GROUP]
                + total[s * 2 * GROUP + GROUP : (s + 1) * 2 * GROUP]
            )
        first = slots * 2 * GROUP + o * chunks
        outbox[o, chunks * GROUP :] = jnp.zeros((outbox.shape[1] - chunks * GROUP, LANES), jnp.float32)
        outbox[o, chunks * GROUP : chunks * GROUP + chunks] = total[first : first + chunks]

    trades = []
    for shift in range(1, peers):
        peer = lax.rem(places[0] + shift, peers)
        trades.append(
            pltpu.make_async_remote_copy(
                src_ref=outbox.at[peer],
                dst_ref=inbox.at[shift - 1],
                send_sem=trade_send.at[shift - 1],
                recv_sem=trade_recv.at[shift - 1],
                device_id={"gx": peer},
                device_id_type=MESH,
            )
        )
    for trade in trades:
        trade.start()
    for load in loads[5:]:
        load.wait()
    for trade in trades:
        trade.wait_recv()

    point = lax.broadcasted_iota(jnp.int32, (GROUP, LANES), 0)
    bits = [(point // size) % 2 for size in (4, 2, 1)]

    def partner(value, axis):
        size = (4, 2, 1)[axis]
        if size * 2 == GROUP:
            return pltpu.roll(value, size, 0)
        return jnp.where(
            bits[axis] == 0, pltpu.roll(value, GROUP - size, 0), pltpu.roll(value, size, 0)
        )

    near = 0.5 + 0.5 / math.sqrt(3.0)
    far = 0.5 - 0.5 / math.sqrt(3.0)
    signs = [bits[axis].astype(jnp.float32) * 2.0 - 1.0 for axis in range(3)]

    def shaped(value, axis):
        return near * value + far * partner(value, axis)

    def sloped(value, axis):
        return signs[axis] * (value + partner(value, axis))

    for k in range(chunks):
        at = slice(k * LANES, (k + 1) * LANES)
        own = pl.ds(k * GROUP, GROUP)
        sums = outbox[places[0], own]
        count = outbox[places[0], pl.ds(chunks * GROUP + k, 1)]
        for shift in range(1, peers):
            sums = sums + inbox[shift - 1, own]
            count = count + inbox[shift - 1, pl.ds(chunks * GROUP + k, 1)]
        thermal = sums / jnp.maximum(count, 1.0)
        normal = [strain[d, :, at] - expansion * thermal for d in range(3)]
        volume = normal[0] + normal[1] + normal[2]
        trial = [
            stress[d, :, at] + lame_first * volume + (2.0 * shear_modulus) * normal[d] for d in range(3)
        ]
        shear = [stress[d, :, at] + (2.0 * shear_modulus) * strain[d, :, at] for d in range(3, 6)]
        pressure = (trial[0] + trial[1] + trial[2]) / 3.0
        deviator = [value - pressure for value in trial]
        squares = (
            deviator[0] * deviator[0] + deviator[1] * deviator[1] + deviator[2] * deviator[2]
        ) + 2.0 * (shear[0] * shear[0] + shear[1] * shear[1] + shear[2] * shear[2])
        equivalent = jnp.sqrt(1.5 * squares)
        bound = limit[0:1, at]
        plastic = jnp.maximum(equivalent - bound, 0.0) / (3.0 * shear_modulus + hardening)
        factor = 1.0 - 3.0 * shear_modulus * plastic / jnp.maximum(equivalent, bound)
        result = [pressure + factor * value for value in deviator] + [factor * value for value in shear]
        for d in range(6):
            new_stress[d, :, at] = result[d]
        picks = [[0, 5, 4], [5, 1, 3], [4, 3, 2]]
        for c in range(3):
            fx, fy, fz = (result[d] * 0.125 for d in picks[c])
            plane = shaped(sloped(fx, 0) , 1) + sloped(shaped(fy, 0), 1)
            new_forces[c, :, at] = shaped(plane, 2) + sloped(shaped(shaped(fz, 0), 1), 2)

    write_stress = pltpu.make_async_copy(new_stress, stress_out, out_sems.at[1])
    write_forces = pltpu.make_async_copy(new_forces, forces_out, out_sems.at[2])
    write_stress.start()
    write_forces.start()
    for trade in trades:
        trade.wait_send()
    for step in range(STEPS):
        for axis in range(3):
            for up, exists in ((False, has_lower[axis]), (True, has_upper[axis])):

                @pl.when(exists)
                def _(step=step, axis=axis, up=up):
                    halo(step, axis, up).wait_send()

    write_temp.wait()
    write_stress.wait()
    write_forces.wait()


def local(
    counts_of,
    nodal_warmth_degrees,
    thermal_transfer_coefficient,
    taken_beam_fraction,
    laid_tiers,
    holding_brick_column,
    piece_onto_solid_brick,
    deformation_change,
    earlier_tension_state,
    plastic_onset_threshold,
):
    block = thermal_transfer_coefficient.shape
    size_x, size_y, size_z = block
    rows = size_x * size_y
    cells = deformation_change.shape[2]
    assert size_z == LANES and rows % GROUP == 0 and cells % LANES == 0
    chunks = cells // LANES
    peers = counts_of[0]
    slots = peers * chunks
    box = (chunks * GROUP + -(-chunks // GROUP) * GROUP, LANES)
    flat = (rows, LANES)
    f32 = jnp.float32
    anywhere = pl.BlockSpec(memory_space=pl.ANY)
    vmem = pltpu.VMEM
    temp, stress, forces = pl.pallas_call(
        functools.partial(kernel, block, counts_of, cells),
        out_shape=(
            jax.ShapeDtypeStruct((27 * rows, LANES), f32),
            jax.ShapeDtypeStruct(earlier_tension_state.shape, f32),
            jax.ShapeDtypeStruct((3, 8, cells), f32),
        ),
        in_specs=[pl.BlockSpec(memory_space=pltpu.SMEM)] + [anywhere] * 8,
        out_specs=(anywhere,) * 3,
        scratch_shapes=[
            vmem((27 * rows, LANES), f32),
            vmem(flat, f32),
            vmem(flat, f32),
            vmem(flat, jnp.int32),
            vmem(flat, jnp.int32),
            vmem(deformation_change.shape, f32),
            vmem(earlier_tension_state.shape, f32),
            vmem((1, cells), f32),
            vmem((27 * rows, LANES), f32),
            vmem((27 * rows, LANES), f32),
            vmem((STEPS, 2, 10 * size_y, LANES), f32),
            vmem((STEPS, 2, 10 * size_x, LANES), f32),
            vmem((STEPS, 2, rows, LANES), f32),
            vmem((STEPS, 2, 10 * size_y, LANES), f32),
            vmem((STEPS, 2, 10 * size_x, LANES), f32),
            vmem((STEPS, 2, rows, LANES), f32),
            vmem((GROUP * rows, LANES), f32),
            vmem((slots * 2 * GROUP + slots, rows * LANES), jnp.bfloat16),
            vmem((LANES, rows * LANES), jnp.bfloat16),
            vmem((peers,) + box, f32),
            vmem((max(peers - 1, 1),) + box, f32),
            vmem(earlier_tension_state.shape, f32),
            vmem((3, 8, cells), f32),
            pltpu.SemaphoreType.DMA((8,)),
            pltpu.SemaphoreType.DMA((3,)),
            pltpu.SemaphoreType.DMA((STEPS * 6,)),
            pltpu.SemaphoreType.DMA((STEPS * 6,)),
            pltpu.SemaphoreType.DMA((max(peers - 1, 1),)),
            pltpu.SemaphoreType.DMA((max(peers - 1, 1),)),
        ],
        compiler_params=pltpu.CompilerParams(collective_id=0, has_side_effects=True),
        name="slab",
    )(
        laid_tiers.reshape(1, 1),
        nodal_warmth_degrees.reshape(27 * rows, LANES),
        thermal_transfer_coefficient.reshape(flat),
        taken_beam_fraction.reshape(flat),
        holding_brick_column.reshape(flat),
        piece_onto_solid_brick.reshape(flat),
        deformation_change,
        earlier_tension_state,
        plastic_onset_threshold.reshape(1, cells),
    )
    return temp.reshape(nodal_warmth_degrees.shape), stress, forces


def solution(mesh):
    placed = (
        P(None, None, None, "gx", "gy", "gz"),
        P("gx", "gy", "gz"),
        P("gx", "gy", "gz"),
        P("gx", "gy", "gz"),
        P("gx", "gy", "gz", None, None),
        P("gx", "gy", "gz", None),
        P(None, None, ("gx", "gy", "gz")),
        P(None, None, ("gx", "gy", "gz")),
        P(("gx", "gy", "gz")),
    )
    counts_of = tuple(mesh.shape[name] for name in ("gx", "gy", "gz"))
    return jax.shard_map(
        functools.partial(local, counts_of),
        mesh=mesh,
        in_specs=placed,
        out_specs=(
            P(None, None, None, "gx", "gy", "gz"),
            P(None, None, ("gx", "gy", "gz")),
            P(None, None, ("gx", "gy", "gz")),
        ),
        check_vma=False,
    )
```

```python
import functools
import math

import jax
import jax.numpy as jnp
from jax import lax
from jax.experimental import pallas as pl
from jax.experimental.pallas import tpu as pltpu
from jax.sharding import PartitionSpec as P

STEPS = 4

time_step = 0.003
penalty = 3.0
heat_power = 100.0
expansion = 0.02
shear_modulus = 100.0 / 2.6
lame_first = 30.0 / 0.52
hardening = 10.0
LANES = 128
GROUP = 8
MESH = pl.DeviceIdType.MESH


def face_planes(axis, side):
    planes = []
    for first in range(3):
        for second in range(3):
            index = [first, second]
            index.insert(axis, side)
            planes.append(9 * index[0] + 3 * index[1] + index[2])
    return planes


def gauss_rows():
    half = 0.5 / math.sqrt(3.0)
    return [
        [2.0 * (g - 0.5) * (g - 1.0), -4.0 * g * (g - 1.0), 2.0 * g * (g - 0.5)]
        for g in (0.5 - half, 0.5 + half)
    ]


def pair_coefficient(own, beside):
    scale = time_step * penalty * 2.0 * 6.0
    return scale * own * beside / jnp.maximum(own + beside, 1.0)


def kernel(
    block,
    counts_of,
    cells,
    tiers_hbm,
    warm_hbm,
    cond_hbm,
    beam_hbm,
    owner_hbm,
    piece_hbm,
    strain_hbm,
    stress_hbm,
    limit_hbm,
    pong,
    new_stress,
    new_forces,
    tiers,
    warm,
    cond,
    beam,
    owner,
    piece,
    strain,
    stress,
    limit,
    ping,
    send_x,
    send_y,
    send_z,
    got_x,
    got_y,
    got_z,
    points,
    spread,
    hot,
    outbox,
    inbox,
    in_sems,
    halo_send,
    halo_recv,
    trade_send,
    trade_recv,
):
    size_x, size_y, size_z = block
    rows = size_x * size_y
    names = ("gx", "gy", "gz")
    places = tuple(lax.axis_index(name) for name in names)
    has_lower = tuple(place > 0 for place in places)
    has_upper = tuple(place < count - 1 for place, count in zip(places, counts_of))
    peers = counts_of[0]
    chunks = cells // LANES
    slots = peers * chunks

    loads = [
        pltpu.make_async_copy(source, target, in_sems.at[index])
        for index, (source, target) in enumerate(
            (
                (tiers_hbm, tiers),
                (warm_hbm, warm),
                (cond_hbm, cond),
                (beam_hbm, beam),
                (owner_hbm, owner),
                (piece_hbm, piece),
                (strain_hbm, strain),
                (stress_hbm, stress),
                (limit_hbm, limit),
            )
        )
    ]
    for load in loads:
        load.start()

    barrier = pltpu.get_barrier_semaphore()
    greet_all = peers - 1 > STEPS + 1
    if greet_all:
        for shift in range(1, peers):
            pl.semaphore_signal(
                barrier,
                inc=1,
                device_id={"gx": lax.rem(places[0] + shift, peers)},
                device_id_type=MESH,
            )
    for axis in (1, 2) if greet_all else (0, 1, 2):
        for exists, move in ((has_lower[axis], -1), (has_upper[axis], 1)):

            @pl.when(exists)
            def _(axis=axis, move=move):
                pl.semaphore_signal(
                    barrier, inc=1, device_id={names[axis]: places[axis] + move}, device_id_type=MESH
                )

    sends = (send_x, send_y, send_z)
    gots = (got_x, got_y, got_z)

    for axis in range(3):
        for exists, side in ((has_lower[axis], 0), (has_upper[axis], 1)):

            @pl.when(jnp.logical_not(exists))
            def _(axis=axis, side=side):
                gots[axis][:, side] = jnp.zeros(gots[axis].shape[:1] + gots[axis].shape[2:], jnp.float32)

    def halo(step, axis, up):
        index = (step * 3 + axis) * 2
        target = places[axis] + (1 if up else -1)
        return pltpu.make_async_remote_copy(
            src_ref=sends[axis].at[step, 1 if up else 0],
            dst_ref=gots[axis].at[step, 0 if up else 1],
            send_sem=halo_send.at[index + (1 if up else 0)],
            recv_sem=halo_recv.at[index + (0 if up else 1)],
            device_id={names[axis]: target},
            device_id_type=MESH,
        )

    lane = lax.broadcasted_iota(jnp.int32, (rows, LANES), 1)
    row = lax.broadcasted_iota(jnp.int32, (rows, LANES), 0)
    row_x = row // size_y
    row_y = row - row_x * size_y

    for load in loads[:4]:
        load.wait()
    mask = (lane < tiers[0, 0, 0]).astype(jnp.float32)
    flow = cond[...] * mask

    send_x[0, 0, 9 * size_y : 10 * size_y] = flow[:size_y]
    send_x[0, 1, 9 * size_y : 10 * size_y] = flow[rows - size_y :]
    hold = pong
    hold[0:rows] = flow
    send_y[0, 0, 9 * size_x : 10 * size_x] = hold[pl.ds(0, size_x, stride=size_y)]
    send_y[0, 1, 9 * size_x : 10 * size_x] = hold[pl.ds(size_y - 1, size_x, stride=size_y)]

    neighbours = peers - 1 if greet_all else 0
    for axis in (1, 2) if greet_all else (0, 1, 2):
        neighbours = neighbours + has_lower[axis].astype(jnp.int32) + has_upper[axis].astype(jnp.int32)

    def pack(current, step):
        for side, face in ((0, 0), (1, 2)):
            first = 0 if side == 0 else rows - size_y
            for v, plane in enumerate(face_planes(0, face)):
                send_x[step, side, v * size_y : (v + 1) * size_y] = current[
                    plane * rows + first : plane * rows + first + size_y
                ]
            first = 0 if side == 0 else size_y - 1
            for v, plane in enumerate(face_planes(1, face)):
                send_y[step, side, v * size_x : (v + 1) * size_x] = current[
                    pl.ds(plane * rows + first, size_x, stride=size_y)
                ]
            first = 0 if side == 0 else LANES - 1
            packed = None
            for v, plane in enumerate(face_planes(2, face)):
                value = current[plane * rows : (plane + 1) * rows]
                shift = (v - first) % LANES
                value = pltpu.roll(value, shift, 1) if shift else value
                packed = value if packed is None else jnp.where(lane == v, value, packed)
            if step == 0:
                shift = (9 - first) % LANES
                packed = jnp.where(lane == 9, pltpu.roll(flow, shift, 1), packed)
            send_z[step, side] = packed

    def start(step):
        for axis in range(3):
            for up, exists in ((False, has_lower[axis]), (True, has_upper[axis])):

                @pl.when(exists)
                def _(axis=axis, up=up):
                    halo(step, axis, up).start()

    def arrive(step):
        for axis in range(3):
            for up, exists in ((False, has_upper[axis]), (True, has_lower[axis])):

                @pl.when(exists)
                def _(axis=axis, up=up):
                    halo(step, axis, up).wait_recv()

    pack(warm, 0)
    pl.semaphore_wait(barrier, neighbours)
    start(0)

    def inner(value, axis):
        if axis == 0:
            down, up = pltpu.roll(value, size_y, 0), pltpu.roll(value, rows - size_y, 0)
            low, high = row_x == 0, row_x == size_x - 1
        elif axis == 1:
            down, up = pltpu.roll(value, 1, 0), pltpu.roll(value, rows - 1, 0)
            low, high = row_y == 0, row_y == size_y - 1
        else:
            down, up = pltpu.roll(value, 1, 1), pltpu.roll(value, LANES - 1, 1)
            low, high = lane == 0, lane == LANES - 1
        return (
            jnp.where(low, 0.0, pair_coefficient(value, down)),
            jnp.where(high, 0.0, pair_coefficient(value, up)),
        )

    couples = [inner(flow, axis) for axis in range(3)]
    through = time_step * flow
    extent = [size * count for size, count in zip(block, counts_of)]
    begin = [(place * size) for place, size in zip(places, block)]

    def bell(where, node, centre, near, far):
        offset = where + 0.5 * node - centre
        ratio = offset / jnp.where(offset >= 0.0, near, far)
        return jnp.exp(-3.0 * ratio * ratio)

    where_x = (row_x + begin[0]).astype(jnp.float32)
    where_y = (row_y + begin[1]).astype(jnp.float32)
    where_z = (lane + begin[2]).astype(jnp.float32)
    length, width, height = extent
    heat = (time_step * heat_power * (2.0 / 3.0)) * mask * beam[...]
    bell_y = [bell(where_y, node, width * 0.5, width / 4.0, width / 4.0) for node in range(3)]
    bell_z = [
        heat * bell(where_z, node, height * 0.75, height / 8.0, height / 8.0) for node in range(3)
    ]

    def advance(current, following, step):
        bell_x = [
            bell(
                where_x,
                node,
                length * 0.5 + step * length / 16.0,
                length / 8.0,
                length / 4.0,
            )
            for node in range(3)
        ]
        for part in range(rows // GROUP):
            cut = slice(part * GROUP, (part + 1) * GROUP)
            t = [
                current[plane * rows + part * GROUP : plane * rows + (part + 1) * GROUP]
                for plane in range(27)
            ]
            rate = [None] * 27
            for axis in range(3):
                for v in range(9):
                    p0, p1, p2 = (face_planes(axis, k)[v] for k in range(3))
                    d0, d2 = t[p0] - t[p1], t[p2] - t[p1]
                    both = 2.0 * (d0 + d2)
                    for plane, term in (
                        (p0, both + 12.0 * d0),
                        (p1, -2.0 * both),
                        (p2, both + 12.0 * d2),
                    ):
                        rate[plane] = term if rate[plane] is None else rate[plane] + term
            for a in range(3):
                for b in range(3):
                    beam_ab = bell_x[a][cut] * bell_y[b][cut]
                    for c in range(3):
                        plane = 9 * a + 3 * b + c
                        value = t[plane] - through[cut] * rate[plane] + beam_ab * bell_z[c][cut]
                        following[plane * rows + part * GROUP : plane * rows + (part + 1) * GROUP] = value
        for axis in range(3):
            along = 1 if axis == 2 else 0
            span = LANES if axis == 2 else rows
            shift = (size_y, 1, 1)[axis]
            for p0, p2 in zip(face_planes(axis, 0), face_planes(axis, 2)):
                s0 = slice(p0 * rows, (p0 + 1) * rows)
                s2 = slice(p2 * rows, (p2 + 1) * rows)
                bottom, top = current[s0], current[s2]
                following[s0] += couples[axis][0] * (pltpu.roll(top, shift, along) - bottom)
                following[s2] += couples[axis][1] * (pltpu.roll(bottom, span - shift, along) - top)

    def fix(current, following, step, edges):
        for side, face in ((0, 0), (1, 2)):
            first = 0 if side == 0 else rows - size_y
            for v, plane in enumerate(face_planes(0, face)):
                at = slice(plane * rows + first, plane * rows + first + size_y)
                beside = got_x[step, side, v * size_y : (v + 1) * size_y]
                following[at] += edges[0][side] * (beside - current[at])
            first = 0 if side == 0 else size_y - 1
            for v, plane in enumerate(face_planes(1, face)):
                at = pl.ds(plane * rows + first, size_x, stride=size_y)
                beside = got_y[step, side, v * size_x : (v + 1) * size_x]
                following[at] = following[at] + edges[1][side] * (beside - current[at])
            first = 0 if side == 0 else LANES - 1
            packed = got_z[step, side]
            for v, plane in enumerate(face_planes(2, face)):
                at = slice(plane * rows, (plane + 1) * rows)
                shift = (first - v) % LANES
                beside = pltpu.roll(packed, shift, 1) if shift else packed
                following[at] += edges[2][side] * (beside - current[at])

    def outer_couples():
        points[0:rows] = flow
        edges = []
        edges.append(
            [
                pair_coefficient(
                    flow[first : first + size_y], got_x[0, side, 9 * size_y : 10 * size_y]
                )
                for side, first in ((0, 0), (1, rows - size_y))
            ]
        )
        edges.append(
            [
                pair_coefficient(
                    points[pl.ds(first, size_x, stride=size_y)],
                    got_y[0, side, 9 * size_x : 10 * size_x],
                )
                for side, first in ((0, 0), (1, size_y - 1))
            ]
        )
        edges.append(
            [
                jnp.where(
                    lane == first,
                    pair_coefficient(flow, pltpu.roll(got_z[0, side], (first - 9) % LANES, 1)),
                    0.0,
                )
                for side, first in ((0, 0), (1, LANES - 1))
            ]
        )
        return edges

    def label_rows():
        for load in loads[4:6]:
            load.wait()
        low_iota = lax.broadcasted_iota(jnp.int32, (LANES, LANES), 0)
        slot_iota = lax.broadcasted_iota(jnp.int32, (slots, LANES), 0)
        cell = piece[...]
        chunk = cell // LANES
        low = cell - chunk * LANES
        slot = jnp.where(lane < tiers[0, 0, 0], owner[...] * chunks + chunk, -1)
        for r in range(rows):
            at = slice(r * LANES, (r + 1) * LANES)
            hot[:, at] = (low_iota == low[r : r + 1]).astype(jnp.float32).astype(jnp.bfloat16)
            spread[slots * 2 * GROUP :, at] = (
                (slot_iota == slot[r : r + 1]).astype(jnp.float32).astype(jnp.bfloat16)
            )
        return slot

    slot = None
    edges = None
    current = warm
    for step in range(STEPS):
        following = ping if step % 2 == 0 else pong
        if step > 0:
            pack(current, step)
            start(step)
        advance(current, following, step)
        if step == 0:
            slot = label_rows()
        arrive(step)
        if step == 0:
            edges = outer_couples()
        fix(current, following, step, edges)
        current = following


    table = gauss_rows()
    for part in range(rows // GROUP):
        change = [
            current[p * rows + part * GROUP : p * rows + (part + 1) * GROUP]
            - warm[p * rows + part * GROUP : p * rows + (part + 1) * GROUP]
            for p in range(27)
        ]
        stage = [
            [sum(table[p][a] * change[9 * a + v] for a in range(3)) for v in range(9)] for p in range(2)
        ]
        stage = [
            [
                [sum(table[q][b] * stage[p][3 * b + c] for b in range(3)) for c in range(3)]
                for q in range(2)
            ]
            for p in range(2)
        ]
        for p in range(2):
            for q in range(2):
                for r in range(2):
                    g = 4 * p + 2 * q + r
                    points[g * rows + part * GROUP : g * rows + (part + 1) * GROUP] = sum(
                        table[r][c] * stage[p][q][c] for c in range(3)
                    )

    for r in range(rows):
        at = slice(r * LANES, (r + 1) * LANES)
        value = points[pl.ds(r, GROUP, stride=rows)]
        coarse = value.astype(jnp.bfloat16).astype(jnp.float32)
        both = jnp.concatenate([coarse, value - coarse], axis=0)
        mine = jnp.broadcast_to(slot[r : r + 1], (2 * GROUP, LANES))
        for s in range(slots):
            spread[s * 2 * GROUP : (s + 1) * 2 * GROUP, at] = jnp.where(mine == s, both, 0.0).astype(
                jnp.bfloat16
            )
    total = lax.dot_general(
        spread[...], hot[...], (((1,), (1,)), ((), ())), preferred_element_type=jnp.float32
    )
    for o in range(peers):
        for k in range(chunks):
            s = o * chunks + k
            outbox[o, k * GROUP : (k + 1) * GROUP] = (
                total[s * 2 * GROUP : s * 2 * GROUP + GROUP]
                + total[s * 2 * GROUP + GROUP : (s + 1) * 2 * GROUP]
            )
        first = slots * 2 * GROUP + o * chunks
        outbox[o, chunks * GROUP :] = jnp.zeros((outbox.shape[1] - chunks * GROUP, LANES), jnp.float32)
        outbox[o, chunks * GROUP : chunks * GROUP + chunks] = total[first : first + chunks]

    trades = []
    for shift in range(1, peers):
        peer = lax.rem(places[0] + shift, peers)
        trades.append(
            pltpu.make_async_remote_copy(
                src_ref=outbox.at[peer],
                dst_ref=inbox.at[shift - 1],
                send_sem=trade_send.at[shift - 1],
                recv_sem=trade_recv.at[shift - 1],
                device_id={"gx": peer},
                device_id_type=MESH,
            )
        )
    for trade in trades:
        trade.start()
    for load in loads[6:]:
        load.wait()
    for trade in trades:
        trade.wait_recv()

    point = lax.broadcasted_iota(jnp.int32, (GROUP, LANES), 0)
    bits = [(point // size) % 2 for size in (4, 2, 1)]

    def partner(value, axis):
        size = (4, 2, 1)[axis]
        if size * 2 == GROUP:
            return pltpu.roll(value, size, 0)
        return jnp.where(
            bits[axis] == 0, pltpu.roll(value, GROUP - size, 0), pltpu.roll(value, size, 0)
        )

    near = 0.5 + 0.5 / math.sqrt(3.0)
    far = 0.5 - 0.5 / math.sqrt(3.0)
    signs = [bits[axis].astype(jnp.float32) * 2.0 - 1.0 for axis in range(3)]

    def shaped(value, axis):
        return near * value + far * partner(value, axis)

    def sloped(value, axis):
        return signs[axis] * (value + partner(value, axis))

    for k in range(chunks):
        at = slice(k * LANES, (k + 1) * LANES)
        own = pl.ds(k * GROUP, GROUP)
        sums = outbox[places[0], own]
        count = outbox[places[0], pl.ds(chunks * GROUP + k, 1)]
        for shift in range(1, peers):
            sums = sums + inbox[shift - 1, own]
            count = count + inbox[shift - 1, pl.ds(chunks * GROUP + k, 1)]
        thermal = sums / jnp.maximum(count, 1.0)
        normal = [strain[d, :, at] - expansion * thermal for d in range(3)]
        volume = normal[0] + normal[1] + normal[2]
        trial = [
            stress[d, :, at] + lame_first * volume + (2.0 * shear_modulus) * normal[d] for d in range(3)
        ]
        shear = [stress[d, :, at] + (2.0 * shear_modulus) * strain[d, :, at] for d in range(3, 6)]
        pressure = (trial[0] + trial[1] + trial[2]) / 3.0
        deviator = [value - pressure for value in trial]
        squares = (
            deviator[0] * deviator[0] + deviator[1] * deviator[1] + deviator[2] * deviator[2]
        ) + 2.0 * (shear[0] * shear[0] + shear[1] * shear[1] + shear[2] * shear[2])
        equivalent = jnp.sqrt(1.5 * squares)
        bound = limit[0:1, at]
        plastic = jnp.maximum(equivalent - bound, 0.0) / (3.0 * shear_modulus + hardening)
        factor = 1.0 - 3.0 * shear_modulus * plastic / jnp.maximum(equivalent, bound)
        result = [pressure + factor * value for value in deviator] + [factor * value for value in shear]
        for d in range(6):
            new_stress[d, :, at] = result[d]
        picks = [[0, 5, 4], [5, 1, 3], [4, 3, 2]]
        for c in range(3):
            fx, fy, fz = (result[d] * 0.125 for d in picks[c])
            plane = shaped(sloped(fx, 0) , 1) + sloped(shaped(fy, 0), 1)
            new_forces[c, :, at] = shaped(plane, 2) + sloped(shaped(shaped(fz, 0), 1), 2)

    for trade in trades:
        trade.wait_send()
    for step in range(STEPS):
        for axis in range(3):
            for up, exists in ((False, has_lower[axis]), (True, has_upper[axis])):

                @pl.when(exists)
                def _(step=step, axis=axis, up=up):
                    halo(step, axis, up).wait_send()


def write_out(temp, stress, forces, temp_out, stress_out, forces_out, sems):
    copies = [
        pltpu.make_async_copy(source, target, sems.at[index])
        for index, (source, target) in enumerate(
            ((temp, temp_out), (stress, stress_out), (forces, forces_out))
        )
    ]
    for copy in copies:
        copy.start()
    for copy in copies:
        copy.wait()


def local(
    counts_of,
    nodal_warmth_degrees,
    thermal_transfer_coefficient,
    taken_beam_fraction,
    laid_tiers,
    holding_brick_column,
    piece_onto_solid_brick,
    deformation_change,
    earlier_tension_state,
    plastic_onset_threshold,
):
    block = thermal_transfer_coefficient.shape
    size_x, size_y, size_z = block
    rows = size_x * size_y
    cells = deformation_change.shape[2]
    assert size_z == LANES and rows % GROUP == 0 and cells % LANES == 0
    chunks = cells // LANES
    peers = counts_of[0]
    slots = peers * chunks
    box = (chunks * GROUP + -(-chunks // GROUP) * GROUP, LANES)
    flat = (rows, LANES)
    f32 = jnp.float32
    anywhere = pl.BlockSpec(memory_space=pl.ANY)
    vmem = pltpu.VMEM
    shapes = ((27 * rows, LANES), earlier_tension_state.shape, (3, 8, cells))
    inside = pl.BlockSpec(memory_space=vmem)
    results = pl.pallas_call(
        functools.partial(kernel, block, counts_of, cells),
        out_shape=tuple(vmem(shape, f32) for shape in shapes),
        in_specs=[pl.BlockSpec(memory_space=pltpu.HBM)] + [anywhere] * 8,
        out_specs=(inside,) * 3,
        scratch_shapes=[
            pltpu.SMEM((1, 1, 1), jnp.int32),
            vmem((27 * rows, LANES), f32),
            vmem(flat, f32),
            vmem(flat, f32),
            vmem(flat, jnp.int32),
            vmem(flat, jnp.int32),
            vmem(deformation_change.shape, f32),
            vmem(earlier_tension_state.shape, f32),
            vmem((1, cells), f32),
            vmem((27 * rows, LANES), f32),
            vmem((STEPS, 2, 10 * size_y, LANES), f32),
            vmem((STEPS, 2, 10 * size_x, LANES), f32),
            vmem((STEPS, 2, rows, LANES), f32),
            vmem((STEPS, 2, 10 * size_y, LANES), f32),
            vmem((STEPS, 2, 10 * size_x, LANES), f32),
            vmem((STEPS, 2, rows, LANES), f32),
            vmem((GROUP * rows, LANES), f32),
            vmem((slots * 2 * GROUP + slots, rows * LANES), jnp.bfloat16),
            vmem((LANES, rows * LANES), jnp.bfloat16),
            vmem((peers,) + box, f32),
            vmem((max(peers - 1, 1),) + box, f32),
            pltpu.SemaphoreType.DMA((9,)),
            pltpu.SemaphoreType.DMA((STEPS * 6,)),
            pltpu.SemaphoreType.DMA((STEPS * 6,)),
            pltpu.SemaphoreType.DMA((max(peers - 1, 1),)),
            pltpu.SemaphoreType.DMA((max(peers - 1, 1),)),
        ],
        compiler_params=pltpu.CompilerParams(collective_id=0, has_side_effects=True),
        name="slab",
    )(
        laid_tiers,
        nodal_warmth_degrees.reshape(27 * rows, LANES),
        thermal_transfer_coefficient.reshape(flat),
        taken_beam_fraction.reshape(flat),
        holding_brick_column.reshape(flat),
        piece_onto_solid_brick.reshape(flat),
        deformation_change,
        earlier_tension_state,
        plastic_onset_threshold.reshape(1, cells),
    )
    temp, stress, forces = pl.pallas_call(
        write_out,
        out_shape=tuple(jax.ShapeDtypeStruct(shape, f32) for shape in shapes),
        in_specs=[inside] * 3,
        out_specs=(anywhere,) * 3,
        scratch_shapes=[pltpu.SemaphoreType.DMA((3,))],
        name="write_out",
    )(*(pltpu.with_memory_space_constraint(result, vmem) for result in results))
    return temp.reshape(nodal_warmth_degrees.shape), stress, forces


def solution(mesh):
    placed = (
        P(None, None, None, "gx", "gy", "gz"),
        P("gx", "gy", "gz"),
        P("gx", "gy", "gz"),
        P("gx", "gy", "gz"),
        P("gx", "gy", "gz", None, None),
        P("gx", "gy", "gz", None),
        P(None, None, ("gx", "gy", "gz")),
        P(None, None, ("gx", "gy", "gz")),
        P(("gx", "gy", "gz")),
    )
    counts_of = tuple(mesh.shape[name] for name in ("gx", "gy", "gz"))
    return jax.shard_map(
        functools.partial(local, counts_of),
        mesh=mesh,
        in_specs=placed,
        out_specs=(
            P(None, None, None, "gx", "gy", "gz"),
            P(None, None, ("gx", "gy", "gz")),
            P(None, None, ("gx", "gy", "gz")),
        ),
        check_vma=False,
    )
```

```python
import functools
import math

import jax
import jax.numpy as jnp
from jax import lax
from jax.experimental import pallas as pl
from jax.experimental.pallas import tpu as pltpu
from jax.sharding import PartitionSpec as P

STEPS = 4
PAIRS = STEPS // 2

time_step = 0.003
penalty = 3.0
heat_power = 100.0
expansion = 0.02
shear_modulus = 100.0 / 2.6
lame_first = 30.0 / 0.52
hardening = 10.0
LANES = 128
GROUP = 8
MESH = pl.DeviceIdType.MESH


def face_planes(axis, side):
    planes = []
    for first in range(3):
        for second in range(3):
            index = [first, second]
            index.insert(axis, side)
            planes.append(9 * index[0] + 3 * index[1] + index[2])
    return planes


def gauss_rows():
    half = 0.5 / math.sqrt(3.0)
    return [
        [2.0 * (g - 0.5) * (g - 1.0), -4.0 * g * (g - 1.0), 2.0 * g * (g - 0.5)]
        for g in (0.5 - half, 0.5 + half)
    ]


def pair_coefficient(own, beside):
    scale = time_step * penalty * 2.0 * 6.0
    return scale * own * beside / jnp.maximum(own + beside, 1.0)


def kernel(
    block,
    counts_of,
    cells,
    tiers_hbm,
    warm_hbm,
    cond_hbm,
    beam_hbm,
    owner_hbm,
    piece_hbm,
    strain_hbm,
    stress_hbm,
    limit_hbm,
    pong,
    new_stress,
    new_forces,
    tiers,
    warm,
    cond,
    beam,
    owner,
    piece,
    strain,
    stress,
    limit,
    ping,
    send_x,
    send_y,
    send_z,
    got_x,
    got_y,
    got_z,
    corner_out,
    corner_in,
    points,
    spread,
    hot,
    tally,
    outbox,
    inbox,
    count_out,
    count_in,
    in_sems,
    halo_send,
    halo_recv,
    trade_send,
    trade_recv,
    wide,
    count_send,
    count_recv,
    corner_send,
    corner_recv,
):
    size_x, size_y, size_z = block
    rows = size_x * size_y
    names = ("gx", "gy", "gz")
    places = tuple(lax.axis_index(name) for name in names)
    has_lower = tuple(place > 0 for place in places)
    has_upper = tuple(place < count - 1 for place, count in zip(places, counts_of))
    peers = counts_of[0]
    chunks = cells // LANES
    slots = peers * chunks

    third = 9 * size_x * size_y
    loads = [
        pltpu.make_async_copy(source, target, in_sems.at[index])
        for index, (source, target) in enumerate(
            (
                (tiers_hbm, tiers),
                *(
                    (warm_hbm.at[a * third : (a + 1) * third], warm.at[a * third : (a + 1) * third])
                    for a in range(3)
                ),
                (cond_hbm, cond),
                (beam_hbm, beam),
                (owner_hbm, owner),
                (piece_hbm, piece),
                (strain_hbm, strain),
                (stress_hbm, stress),
                (limit_hbm, limit),
            )
        )
    ]
    for load in loads:
        load.start()

    barrier = pltpu.get_barrier_semaphore()
    greet_all = peers - 1 > PAIRS + 1
    if greet_all:
        for shift in range(1, peers):
            pl.semaphore_signal(
                barrier,
                inc=1,
                device_id={"gx": lax.rem(places[0] + shift, peers)},
                device_id_type=MESH,
            )
    for axis in (1, 2) if greet_all else (0, 1, 2):
        for exists, move in ((has_lower[axis], -1), (has_upper[axis], 1)):

            @pl.when(exists)
            def _(axis=axis, move=move):
                pl.semaphore_signal(
                    barrier, inc=1, device_id={names[axis]: places[axis] + move}, device_id_type=MESH
                )

    exists_at = tuple(zip(has_lower, has_upper))
    corners = []
    for kind, (first, second) in enumerate(((0, 1), (0, 2), (1, 2))):
        for s in range(2):
            for t in range(2):
                both = jnp.logical_and(exists_at[first][s], exists_at[second][t])
                place = {
                    names[first]: places[first] + 2 * s - 1,
                    names[second]: places[second] + 2 * t - 1,
                }
                corners.append((4 * kind + 2 * s + t, 4 * kind + 3 - 2 * s - t, both, place))

    for out_slot, _, both, place in corners:

        @pl.when(both)
        def _(place=place):
            pl.semaphore_signal(barrier, inc=1, device_id=place, device_id_type=MESH)

        @pl.when(jnp.logical_not(both))
        def _(out_slot=out_slot):
            corner_in[:, out_slot] = jnp.zeros(
                corner_in.shape[:1] + corner_in.shape[2:], jnp.float32
            )

    sends = (send_x, send_y, send_z)
    gots = (got_x, got_y, got_z)

    for axis in range(3):
        for exists, side in ((has_lower[axis], 0), (has_upper[axis], 1)):

            @pl.when(jnp.logical_not(exists))
            def _(axis=axis, side=side):
                gots[axis][:, side] = jnp.zeros(gots[axis].shape[:1] + gots[axis].shape[2:], jnp.float32)

    def halo(step, axis, up):
        index = (step * 3 + axis) * 2
        target = places[axis] + (1 if up else -1)
        return pltpu.make_async_remote_copy(
            src_ref=sends[axis].at[step, 1 if up else 0],
            dst_ref=gots[axis].at[step, 0 if up else 1],
            send_sem=halo_send.at[index + (1 if up else 0)],
            recv_sem=halo_recv.at[index + (0 if up else 1)],
            device_id={names[axis]: target},
            device_id_type=MESH,
        )

    lane = lax.broadcasted_iota(jnp.int32, (rows, LANES), 1)
    row = lax.broadcasted_iota(jnp.int32, (rows, LANES), 0)
    row_x = row // size_y
    row_y = row - row_x * size_y

    for load in loads[:6]:
        load.wait()
    mask = (lane < tiers[0, 0, 0]).astype(jnp.float32)
    flow = cond[...] * mask

    send_x[0, 0, 9 * size_y : 10 * size_y] = flow[:size_y]
    send_x[0, 1, 9 * size_y : 10 * size_y] = flow[rows - size_y :]
    hold = pong
    hold[0:rows] = flow
    send_y[0, 0, 9 * size_x : 10 * size_x] = hold[pl.ds(0, size_x, stride=size_y)]
    send_y[0, 1, 9 * size_x : 10 * size_x] = hold[pl.ds(size_y - 1, size_x, stride=size_y)]

    neighbours = peers - 1 if greet_all else 0
    for axis in (1, 2) if greet_all else (0, 1, 2):
        neighbours = neighbours + has_lower[axis].astype(jnp.int32) + has_upper[axis].astype(jnp.int32)

    for _, _, both, _ in corners:
        neighbours = neighbours + both.astype(jnp.int32)

    def corner(pair, out_slot, in_slot, place):
        return pltpu.make_async_remote_copy(
            src_ref=corner_out.at[pair, out_slot],
            dst_ref=corner_in.at[pair, in_slot],
            send_sem=corner_send.at[pair * 12 + out_slot],
            recv_sem=corner_recv.at[pair * 12 + in_slot],
            device_id=place,
            device_id_type=MESH,
        )

    def pack_corners(current, pair):
        for s in range(2):
            for t in range(2):
                r = (0, rows - size_y)[s] + (0, size_y - 1)[t]
                for c in range(3):
                    at = (18 * s + 6 * t + c) * rows + r
                    corner_out[pair, 2 * s + t, c : c + 1] = current[at : at + 1]
                corner_out[pair, 2 * s + t, 3:4] = flow[r : r + 1]
                edge = (0, LANES - 1)[t]
                for kind in (1, 2):
                    count = (size_y, size_x)[kind - 1]
                    packed = None
                    for n in range(4):
                        if kind == 1:
                            first = (0, rows - size_y)[s]
                            if n == 3:
                                value = flow[first : first + size_y]
                            else:
                                first = (18 * s + 3 * n + 2 * t) * rows + first
                                value = current[first : first + size_y]
                        else:
                            first = (0, size_y - 1)[s]
                            if n == 3:
                                value = points[pl.ds(first, size_x, stride=size_y)]
                            else:
                                first = (9 * n + 6 * s + 2 * t) * rows + first
                                value = current[pl.ds(first, size_x, stride=size_y)]
                        shift = (n - edge) % LANES
                        value = pltpu.roll(value, shift, 1) if shift else value
                        packed = value if packed is None else jnp.where(lane[:count] == n, value, packed)
                    corner_out[pair, 4 * kind + 2 * s + t, 0:count] = packed

    def start_corners(pair):
        for out_slot, in_slot, both, place in corners:

            @pl.when(both)
            def _(out_slot=out_slot, in_slot=in_slot, place=place):
                corner(pair, out_slot, in_slot, place).start()

    def arrive_corners(pair):
        for out_slot, in_slot, both, place in corners:

            @pl.when(both)
            def _(out_slot=out_slot, in_slot=in_slot, place=place):
                corner(pair, in_slot, out_slot, place).wait_recv()

    def spread_lane(value, index):
        return jnp.broadcast_to(value[:, index : index + 1], value.shape)

    def foresee(pair):
        now, then = 2 * pair, 2 * pair + 1
        for s in range(2):
            for got, sent, axis, count in ((got_x, send_x, 0, size_y), (got_y, send_y, 1, size_x)):
                flow_beside = got[0, s, 9 * count : 10 * count]
                for v in range(9):
                    at = slice(v * count, (v + 1) * count)
                    beside = got[now, s, at]
                    value = got[then, s, at] + edges[axis][s] * (sent[now, s, at] - beside)
                    t = (v % 3) // 2
                    if v % 3 != 1:
                        kind, n = 1 + axis, v // 3
                        far = corner_in[pair, 4 * kind + 2 * s + t, 0:count]
                        far_flow = corner_in[0, 4 * kind + 2 * s + t, 0:count]
                        edge = (0, LANES - 1)[t]
                        near_far = pair_coefficient(flow_beside, spread_lane(far_flow, 3))
                        value = value + jnp.where(
                            lane[:count] == edge, near_far * (spread_lane(far, n) - beside), 0.0
                        )
                    got[then, s, at] = value
                for t in range(2):
                    index = 2 * s + t if axis == 0 else 2 * t + s
                    r = (0, count - 1)[t]
                    weight = pair_coefficient(flow_beside[r : r + 1], corner_in[0, index, 3:4])
                    for c in range(3):
                        at = (6 * t + c) * count + r
                        at = slice(at, at + 1)
                        got[then, s, at] = got[then, s, at] + weight * (
                            corner_in[pair, index, c : c + 1] - got[now, s, at]
                        )
            flow_beside = spread_lane(got_z[0, s], 9)
            own = spread_lane(flow, (0, LANES - 1)[s])
            beside = got_z[now, s]
            got_z[then, s] = got_z[then, s] + pair_coefficient(own, flow_beside) * (
                send_z[now, s] - beside
            )
            wide[...] = flow_beside
            for t in range(2):
                for kind, count in ((1, size_y), (2, size_x)):
                    if kind == 1:
                        first = (0, rows - size_y)[t]
                        at = slice(first, first + size_y)
                        lanes_of = [6 * t + n for n in range(3)]
                    else:
                        at = pl.ds((0, size_y - 1)[t], size_x, stride=size_y)
                        lanes_of = [3 * n + 2 * t for n in range(3)]
                    far = corner_in[pair, 4 * kind + 2 * t + s, 0:count]
                    far_flow = spread_lane(corner_in[0, 4 * kind + 2 * t + s, 0:count], 3)
                    weight = pair_coefficient(wide[at], far_flow)
                    was = got_z.at[now, s][at]
                    change = jnp.zeros((count, LANES), jnp.float32)
                    for n in range(3):
                        change = jnp.where(
                            lane[:count] == lanes_of[n], weight * (spread_lane(far, n) - was), change
                        )
                    target = got_z.at[then, s]
                    target[at] = target[at] + change

    def pack(current, step):
        for side, face in ((0, 0), (1, 2)):
            first = 0 if side == 0 else rows - size_y
            for v, plane in enumerate(face_planes(0, face)):
                send_x[step, side, v * size_y : (v + 1) * size_y] = current[
                    plane * rows + first : plane * rows + first + size_y
                ]
            first = 0 if side == 0 else size_y - 1
            for v, plane in enumerate(face_planes(1, face)):
                send_y[step, side, v * size_x : (v + 1) * size_x] = current[
                    pl.ds(plane * rows + first, size_x, stride=size_y)
                ]
            first = 0 if side == 0 else LANES - 1
            packed = None
            for v, plane in enumerate(face_planes(2, face)):
                value = current[plane * rows : (plane + 1) * rows]
                shift = (v - first) % LANES
                value = pltpu.roll(value, shift, 1) if shift else value
                packed = value if packed is None else jnp.where(lane == v, value, packed)
            if step == 0:
                shift = (9 - first) % LANES
                packed = jnp.where(lane == 9, pltpu.roll(flow, shift, 1), packed)
            send_z[step, side] = packed

    def start(step):
        for axis in range(3):
            for up, exists in ((False, has_lower[axis]), (True, has_upper[axis])):

                @pl.when(exists)
                def _(axis=axis, up=up):
                    halo(step, axis, up).start()

    def arrive(step, axis):
        for up, exists in ((False, has_upper[axis]), (True, has_lower[axis])):

            @pl.when(exists)
            def _(up=up):
                halo(step, axis, up).wait_recv()

    edges = [None] * 3
    points[0:rows] = flow
    pack(warm, 0)
    pl.semaphore_wait(barrier, neighbours)
    start(0)
    pack_corners(warm, 0)
    start_corners(0)

    def inner(value, axis):
        if axis == 0:
            down, up = pltpu.roll(value, size_y, 0), pltpu.roll(value, rows - size_y, 0)
            low, high = row_x == 0, row_x == size_x - 1
        elif axis == 1:
            down, up = pltpu.roll(value, 1, 0), pltpu.roll(value, rows - 1, 0)
            low, high = row_y == 0, row_y == size_y - 1
        else:
            down, up = pltpu.roll(value, 1, 1), pltpu.roll(value, LANES - 1, 1)
            low, high = lane == 0, lane == LANES - 1
        return (
            jnp.where(low, 0.0, pair_coefficient(value, down)),
            jnp.where(high, 0.0, pair_coefficient(value, up)),
        )

    couples = [inner(flow, axis) for axis in range(3)]
    through = time_step * flow
    extent = [size * count for size, count in zip(block, counts_of)]
    begin = [(place * size) for place, size in zip(places, block)]

    def bell(where, node, centre, near, far):
        offset = where + 0.5 * node - centre
        ratio = offset / jnp.where(offset >= 0.0, near, far)
        return jnp.exp(-3.0 * ratio * ratio)

    where_x = (row_x + begin[0]).astype(jnp.float32)
    where_y = (row_y + begin[1]).astype(jnp.float32)
    where_z = (lane + begin[2]).astype(jnp.float32)
    length, width, height = extent
    heat = (time_step * heat_power * (2.0 / 3.0)) * mask * beam[...]
    bell_y = [bell(where_y, node, width * 0.5, width / 4.0, width / 4.0) for node in range(3)]
    bell_z = [
        heat * bell(where_z, node, height * 0.75, height / 8.0, height / 8.0) for node in range(3)
    ]

    def advance(current, following, step):
        bell_x = [
            bell(
                where_x,
                node,
                length * 0.5 + step * length / 16.0,
                length / 8.0,
                length / 4.0,
            )
            for node in range(3)
        ]
        for part in range(rows // GROUP):
            cut = slice(part * GROUP, (part + 1) * GROUP)
            t = [
                current[plane * rows + part * GROUP : plane * rows + (part + 1) * GROUP]
                for plane in range(27)
            ]
            rate = [None] * 27
            for axis in range(3):
                for v in range(9):
                    p0, p1, p2 = (face_planes(axis, k)[v] for k in range(3))
                    d0, d2 = t[p0] - t[p1], t[p2] - t[p1]
                    both = 2.0 * (d0 + d2)
                    for plane, term in (
                        (p0, both + 12.0 * d0),
                        (p1, -2.0 * both),
                        (p2, both + 12.0 * d2),
                    ):
                        rate[plane] = term if rate[plane] is None else rate[plane] + term
            for a in range(3):
                for b in range(3):
                    beam_ab = bell_x[a][cut] * bell_y[b][cut]
                    for c in range(3):
                        plane = 9 * a + 3 * b + c
                        value = t[plane] - through[cut] * rate[plane] + beam_ab * bell_z[c][cut]
                        following[plane * rows + part * GROUP : plane * rows + (part + 1) * GROUP] = value
        for axis in range(3):
            along = 1 if axis == 2 else 0
            span = LANES if axis == 2 else rows
            shift = (size_y, 1, 1)[axis]
            for p0, p2 in zip(face_planes(axis, 0), face_planes(axis, 2)):
                s0 = slice(p0 * rows, (p0 + 1) * rows)
                s2 = slice(p2 * rows, (p2 + 1) * rows)
                bottom, top = current[s0], current[s2]
                following[s0] += couples[axis][0] * (pltpu.roll(top, shift, along) - bottom)
                following[s2] += couples[axis][1] * (pltpu.roll(bottom, span - shift, along) - top)

    def fix(current, following, step, axis, edges):
        for side, face in ((0, 0), (1, 2)):
            packed = got_z[step, side] if axis == 2 else None
            for v, plane in enumerate(face_planes(axis, face)):
                if axis == 0:
                    first = plane * rows + (0 if side == 0 else rows - size_y)
                    at = slice(first, first + size_y)
                    beside = got_x[step, side, v * size_y : (v + 1) * size_y]
                elif axis == 1:
                    at = pl.ds(plane * rows + (0 if side == 0 else size_y - 1), size_x, stride=size_y)
                    beside = got_y[step, side, v * size_x : (v + 1) * size_x]
                else:
                    at = slice(plane * rows, (plane + 1) * rows)
                    shift = ((0 if side == 0 else LANES - 1) - v) % LANES
                    beside = pltpu.roll(packed, shift, 1) if shift else packed
                following[at] = following[at] + edges[side] * (beside - current[at])

    def outer_couples(axis):
        if axis == 0:
            return [
                pair_coefficient(
                    flow[first : first + size_y], got_x[0, side, 9 * size_y : 10 * size_y]
                )
                for side, first in ((0, 0), (1, rows - size_y))
            ]
        if axis == 1:
            return [
                pair_coefficient(
                    points[pl.ds(first, size_x, stride=size_y)],
                    got_y[0, side, 9 * size_x : 10 * size_x],
                )
                for side, first in ((0, 0), (1, size_y - 1))
            ]
        return [
            jnp.where(
                lane == first,
                pair_coefficient(flow, pltpu.roll(got_z[0, side], (first - 9) % LANES, 1)),
                0.0,
            )
            for side, first in ((0, 0), (1, LANES - 1))
        ]

    def label_rows():
        for load in loads[6:8]:
            load.wait()
        low_iota = lax.broadcasted_iota(jnp.int32, (LANES, LANES), 0)
        slot_iota = lax.broadcasted_iota(jnp.int32, (slots, LANES), 0)
        cell = piece[...]
        chunk = cell // LANES
        low = cell - chunk * LANES
        slot = jnp.where(lane < tiers[0, 0, 0], owner[...] * chunks + chunk, -1)
        for r in range(rows):
            at = slice(r * LANES, (r + 1) * LANES)
            hot[:, at] = (low_iota == low[r : r + 1]).astype(jnp.float32).astype(jnp.bfloat16)
            tally[:, at] = (
                (slot_iota == slot[r : r + 1]).astype(jnp.float32).astype(jnp.bfloat16)
            )
        counted = lax.dot_general(
            tally[...], hot[...], (((1,), (1,)), ((), ())), preferred_element_type=jnp.float32
        )
        count_out[...] = jnp.zeros(count_out.shape, jnp.float32)
        for o in range(peers):
            count_out[o, 0:chunks] = counted[o * chunks : (o + 1) * chunks]
        return slot

    def trade_of(source, target, send_sems, recv_sems):
        copies = []
        for shift in range(1, peers):
            peer = lax.rem(places[0] + shift, peers)
            copies.append(
                pltpu.make_async_remote_copy(
                    src_ref=source.at[peer],
                    dst_ref=target.at[shift - 1],
                    send_sem=send_sems.at[shift - 1],
                    recv_sem=recv_sems.at[shift - 1],
                    device_id={"gx": peer},
                    device_id_type=MESH,
                )
            )
        return copies

    count_trades = trade_of(count_out, count_in, count_send, count_recv)
    slot = None
    current = warm
    for pair in range(PAIRS):
        now, then = 2 * pair, 2 * pair + 1
        middle = ping
        if pair > 0:
            pack(current, now)
            start(now)
            pack_corners(current, pair)
            start_corners(pair)
        advance(current, middle, now)
        pack(middle, then)
        start(then)
        if pair == 0:
            slot = label_rows()
        for axis in (2, 0, 1):
            arrive(now, axis)
            if pair == 0:
                edges[axis] = outer_couples(axis)
            fix(current, middle, now, axis, edges[axis])
        advance(middle, pong, then)
        for axis in (2, 0, 1):
            arrive(then, axis)
        arrive_corners(pair)
        if pair == PAIRS - 1:
            for trade in count_trades:
                trade.start()
        foresee(pair)
        for axis in (2, 0, 1):
            fix(middle, pong, then, axis, edges[axis])
        current = pong

    table = gauss_rows()
    for part in range(rows // GROUP):
        change = [
            current[p * rows + part * GROUP : p * rows + (part + 1) * GROUP]
            - warm[p * rows + part * GROUP : p * rows + (part + 1) * GROUP]
            for p in range(27)
        ]
        stage = [
            [sum(table[p][a] * change[9 * a + v] for a in range(3)) for v in range(9)] for p in range(2)
        ]
        stage = [
            [
                [sum(table[q][b] * stage[p][3 * b + c] for b in range(3)) for c in range(3)]
                for q in range(2)
            ]
            for p in range(2)
        ]
        for p in range(2):
            for q in range(2):
                for r in range(2):
                    g = 4 * p + 2 * q + r
                    points[g * rows + part * GROUP : g * rows + (part + 1) * GROUP] = sum(
                        table[r][c] * stage[p][q][c] for c in range(3)
                    )

    for r in range(rows):
        at = slice(r * LANES, (r + 1) * LANES)
        value = points[pl.ds(r, GROUP, stride=rows)]
        coarse = value.astype(jnp.bfloat16).astype(jnp.float32)
        both = jnp.concatenate([coarse, value - coarse], axis=0)
        mine = jnp.broadcast_to(slot[r : r + 1], (2 * GROUP, LANES))
        for s in range(slots):
            spread[s * 2 * GROUP : (s + 1) * 2 * GROUP, at] = jnp.where(mine == s, both, 0.0).astype(
                jnp.bfloat16
            )
    total = lax.dot_general(
        spread[...], hot[...], (((1,), (1,)), ((), ())), preferred_element_type=jnp.float32
    )
    for o in range(peers):
        for k in range(chunks):
            s = o * chunks + k
            outbox[o, k * GROUP : (k + 1) * GROUP] = (
                total[s * 2 * GROUP : s * 2 * GROUP + GROUP]
                + total[s * 2 * GROUP + GROUP : (s + 1) * 2 * GROUP]
            )

    trades = trade_of(outbox, inbox, trade_send, trade_recv)
    for trade in trades:
        trade.start()
    for load in loads[8:]:
        load.wait()
    for trade in trades + count_trades:
        trade.wait_recv()

    point = lax.broadcasted_iota(jnp.int32, (GROUP, LANES), 0)
    bits = [(point // size) % 2 for size in (4, 2, 1)]

    def partner(value, axis):
        size = (4, 2, 1)[axis]
        if size * 2 == GROUP:
            return pltpu.roll(value, size, 0)
        return jnp.where(
            bits[axis] == 0, pltpu.roll(value, GROUP - size, 0), pltpu.roll(value, size, 0)
        )

    near = 0.5 + 0.5 / math.sqrt(3.0)
    far = 0.5 - 0.5 / math.sqrt(3.0)
    signs = [bits[axis].astype(jnp.float32) * 2.0 - 1.0 for axis in range(3)]

    def shaped(value, axis):
        return near * value + far * partner(value, axis)

    def sloped(value, axis):
        return signs[axis] * (value + partner(value, axis))

    for k in range(chunks):
        at = slice(k * LANES, (k + 1) * LANES)
        own = pl.ds(k * GROUP, GROUP)
        sums = outbox[places[0], own]
        count = count_out[places[0], pl.ds(k, 1)]
        for shift in range(1, peers):
            sums = sums + inbox[shift - 1, own]
            count = count + count_in[shift - 1, pl.ds(k, 1)]
        thermal = sums / jnp.maximum(count, 1.0)
        normal = [strain[d, :, at] - expansion * thermal for d in range(3)]
        volume = normal[0] + normal[1] + normal[2]
        trial = [
            stress[d, :, at] + lame_first * volume + (2.0 * shear_modulus) * normal[d] for d in range(3)
        ]
        shear = [stress[d, :, at] + (2.0 * shear_modulus) * strain[d, :, at] for d in range(3, 6)]
        pressure = (trial[0] + trial[1] + trial[2]) / 3.0
        deviator = [value - pressure for value in trial]
        squares = (
            deviator[0] * deviator[0] + deviator[1] * deviator[1] + deviator[2] * deviator[2]
        ) + 2.0 * (shear[0] * shear[0] + shear[1] * shear[1] + shear[2] * shear[2])
        equivalent = jnp.sqrt(1.5 * squares)
        bound = limit[0:1, at]
        plastic = jnp.maximum(equivalent - bound, 0.0) / (3.0 * shear_modulus + hardening)
        factor = 1.0 - 3.0 * shear_modulus * plastic / jnp.maximum(equivalent, bound)
        result = [pressure + factor * value for value in deviator] + [factor * value for value in shear]
        for d in range(6):
            new_stress[d, :, at] = result[d]
        picks = [[0, 5, 4], [5, 1, 3], [4, 3, 2]]
        for c in range(3):
            fx, fy, fz = (result[d] * 0.125 for d in picks[c])
            plane = shaped(sloped(fx, 0) , 1) + sloped(shaped(fy, 0), 1)
            new_forces[c, :, at] = shaped(plane, 2) + sloped(shaped(shaped(fz, 0), 1), 2)

    for trade in trades + count_trades:
        trade.wait_send()
    for pair in range(PAIRS):
        for out_slot, in_slot, both, place in corners:

            @pl.when(both)
            def _(pair=pair, out_slot=out_slot, in_slot=in_slot, place=place):
                corner(pair, out_slot, in_slot, place).wait_send()
    for step in range(STEPS):
        for axis in range(3):
            for up, exists in ((False, has_lower[axis]), (True, has_upper[axis])):

                @pl.when(exists)
                def _(step=step, axis=axis, up=up):
                    halo(step, axis, up).wait_send()


def write_out(temp, stress, forces, temp_out, stress_out, forces_out, sems):
    third = temp.shape[0] // 3
    parts = [pl.ds(a * third, third) for a in range(3)]
    copies = [
        pltpu.make_async_copy(source, target, sems.at[index])
        for index, (source, target) in enumerate(
            (
                *((temp.at[part], temp_out.at[part]) for part in parts),
                (stress, stress_out),
                (forces, forces_out),
            )
        )
    ]
    for copy in copies:
        copy.start()
    for copy in copies:
        copy.wait()


def local(
    counts_of,
    nodal_warmth_degrees,
    thermal_transfer_coefficient,
    taken_beam_fraction,
    laid_tiers,
    holding_brick_column,
    piece_onto_solid_brick,
    deformation_change,
    earlier_tension_state,
    plastic_onset_threshold,
):
    block = thermal_transfer_coefficient.shape
    size_x, size_y, size_z = block
    rows = size_x * size_y
    cells = deformation_change.shape[2]
    assert size_z == LANES and rows % GROUP == 0 and cells % LANES == 0
    chunks = cells // LANES
    peers = counts_of[0]
    slots = peers * chunks
    box = (chunks * GROUP, LANES)
    count_box = (-(-chunks // GROUP) * GROUP, LANES)
    flat = (rows, LANES)
    f32 = jnp.float32
    anywhere = pl.BlockSpec(memory_space=pl.ANY)
    vmem = pltpu.VMEM
    shapes = ((27 * rows, LANES), earlier_tension_state.shape, (3, 8, cells))
    inside = pl.BlockSpec(memory_space=vmem)
    results = pl.pallas_call(
        functools.partial(kernel, block, counts_of, cells),
        out_shape=tuple(vmem(shape, f32) for shape in shapes),
        in_specs=[pl.BlockSpec(memory_space=pltpu.HBM)] + [anywhere] * 8,
        out_specs=(inside,) * 3,
        scratch_shapes=[
            pltpu.SMEM((1, 1, 1), jnp.int32),
            vmem((27 * rows, LANES), f32),
            vmem(flat, f32),
            vmem(flat, f32),
            vmem(flat, jnp.int32),
            vmem(flat, jnp.int32),
            vmem(deformation_change.shape, f32),
            vmem(earlier_tension_state.shape, f32),
            vmem((1, cells), f32),
            vmem((27 * rows, LANES), f32),
            vmem((STEPS, 2, 10 * size_y, LANES), f32),
            vmem((STEPS, 2, 10 * size_x, LANES), f32),
            vmem((STEPS, 2, rows, LANES), f32),
            vmem((STEPS, 2, 10 * size_y, LANES), f32),
            vmem((STEPS, 2, 10 * size_x, LANES), f32),
            vmem((STEPS, 2, rows, LANES), f32),
            vmem((PAIRS, 12, max(4, size_x, size_y), LANES), f32),
            vmem((PAIRS, 12, max(4, size_x, size_y), LANES), f32),
            vmem((GROUP * rows, LANES), f32),
            vmem((slots * 2 * GROUP, rows * LANES), jnp.bfloat16),
            vmem((LANES, rows * LANES), jnp.bfloat16),
            vmem((slots, rows * LANES), jnp.bfloat16),
            vmem((peers,) + box, f32),
            vmem((max(peers - 1, 1),) + box, f32),
            vmem((peers,) + count_box, f32),
            vmem((max(peers - 1, 1),) + count_box, f32),
            pltpu.SemaphoreType.DMA((11,)),
            pltpu.SemaphoreType.DMA((STEPS * 6,)),
            pltpu.SemaphoreType.DMA((STEPS * 6,)),
            pltpu.SemaphoreType.DMA((max(peers - 1, 1),)),
            pltpu.SemaphoreType.DMA((max(peers - 1, 1),)),
            vmem(flat, f32),
            pltpu.SemaphoreType.DMA((max(peers - 1, 1),)),
            pltpu.SemaphoreType.DMA((max(peers - 1, 1),)),
            pltpu.SemaphoreType.DMA((PAIRS * 12,)),
            pltpu.SemaphoreType.DMA((PAIRS * 12,)),
        ],
        compiler_params=pltpu.CompilerParams(collective_id=0, has_side_effects=True),
        name="slab",
    )(
        laid_tiers,
        nodal_warmth_degrees.reshape(27 * rows, LANES),
        thermal_transfer_coefficient.reshape(flat),
        taken_beam_fraction.reshape(flat),
        holding_brick_column.reshape(flat),
        piece_onto_solid_brick.reshape(flat),
        deformation_change,
        earlier_tension_state,
        plastic_onset_threshold.reshape(1, cells),
    )
    temp, stress, forces = pl.pallas_call(
        write_out,
        out_shape=tuple(jax.ShapeDtypeStruct(shape, f32) for shape in shapes),
        in_specs=[inside] * 3,
        out_specs=(anywhere,) * 3,
        scratch_shapes=[pltpu.SemaphoreType.DMA((5,))],
        name="write_out",
    )(*(pltpu.with_memory_space_constraint(result, vmem) for result in results))
    return temp.reshape(nodal_warmth_degrees.shape), stress, forces


def solution(mesh):
    placed = (
        P(None, None, None, "gx", "gy", "gz"),
        P("gx", "gy", "gz"),
        P("gx", "gy", "gz"),
        P("gx", "gy", "gz"),
        P("gx", "gy", "gz", None, None),
        P("gx", "gy", "gz", None),
        P(None, None, ("gx", "gy", "gz")),
        P(None, None, ("gx", "gy", "gz")),
        P(("gx", "gy", "gz")),
    )
    counts_of = tuple(mesh.shape[name] for name in ("gx", "gy", "gz"))
    return jax.shard_map(
        functools.partial(local, counts_of),
        mesh=mesh,
        in_specs=placed,
        out_specs=(
            P(None, None, None, "gx", "gy", "gz"),
            P(None, None, ("gx", "gy", "gz")),
            P(None, None, ("gx", "gy", "gz")),
        ),
        check_vma=False,
    )
```
